256 devices in a mesh: grp: 16 (over z_lo, y, core), dp: 16 (over x, z_hi).
Axes of the slice: x: 4, y: 4, z: 8 (z_hi: 4, z_lo: 2; z = z_hi * 2 + z_lo), core: 2. Of those that a mesh axis runs over, the one named last changes fastest.
Arguments:
- queries: bfloat16 [16, 16, 128, 2048], P('dp', 'grp'), may hold values from -18 to 18
- mem_keys: bfloat16 [16, 16, 256, 2048], P('dp', 'grp'), may hold values from -18 to 18
- mem_values: bfloat16 [16, 16, 256, 2048], P('dp', 'grp'), may hold values from -48 to 48
- lengths: int32 [16, 16], P('dp'), may hold values from 128 to 256, as said below
- mates: int32 [16, 16, 16], P('dp'), may hold values 0 or 1
- out_grad: bfloat16 [16, 16, 128, 2048], P('dp', 'grp'), may hold values from -6 to 6
- mlp_input: bfloat16 [16, 16, 128, 4096], P('dp', 'grp'), may hold values from -6 to 6
- gate_pre: bfloat16 [16, 16, 128, 5632], P('dp', 'grp'), may hold values from -6 to 6
- hidden_grad: bfloat16 [16, 16, 128, 5632], P('dp', 'grp'), may hold values from -0.03125 to 0.03125
Outputs:
- attn_out: bfloat16 [16, 16, 128, 2048], P('dp', 'grp')
- q_grad: bfloat16 [16, 16, 128, 2048], P('dp', 'grp')
- up_grad: float32 [4096, 5632], P(None, ('grp', 'dp'))
The draws below stay inside these ranges and needn't reach their ends.
Inputs may be any that keep to these rules, and one draw needn't show every extreme that they name: `lengths`: each is a multiple of 128; in every group some document has 256. `mates`: A document reads its own previous context whatever its diagonal entry.
All inputs are finite; a program needn't handle non-finite values. No bound on the sum of `mates` on one device may be relied on, other than what follows from the above.
Results may differ from the reference program's by a relative error of at most 0.025.
Values may be sent and summed in bfloat16 or wider, within the bound.
No kernel may reach another device: no remote copies, remote signals or barrier semaphores. Data moves between devices by JAX's collectives and lax.ppermute only.
A program may use at most 128 MiB of HBM per device.

```python
import jax
import jax.numpy as jnp
from jax import lax

D = 4096
HEAD_DIM = 128
HEADS = 16
FF = 5632
BLOCK = 128
MAXMEM = 256
Q = 128
GROUPS = 16
MEMBERS = 16
TOKENS = 32768


def shared_draw(key):
    query_key = jax.random.fold_in(key, 101)
    memory_key = jax.random.fold_in(key, 202)
    query_shape = (GROUPS, MEMBERS, Q, HEADS, HEAD_DIM)
    memory_shape = (GROUPS, MEMBERS, MAXMEM, HEADS, HEAD_DIM)
    query_vals = 1.5 * jnp.clip(jax.random.normal(query_key, query_shape, jnp.float32), -6.0, 6.0)
    memory_vals = jnp.clip(jax.random.normal(memory_key, memory_shape, jnp.float32), -6.0, 6.0)
    query_flat = query_vals.reshape(GROUPS, MEMBERS, Q, HEADS * HEAD_DIM)
    memory_flat = memory_vals.reshape(GROUPS, MEMBERS, MAXMEM, HEADS * HEAD_DIM)
    return (query_flat, memory_flat)


def draw_queries(key, part):
    return shared_draw(key)[0].astype(jnp.bfloat16)


def draw_mem_keys(key, part):
    return shared_draw(key)[1].astype(jnp.bfloat16)


def draw_lengths(key, part):
    granules = jax.random.randint(jax.random.fold_in(key, 7), (GROUPS, MEMBERS), 1, MAXMEM // BLOCK + 1)
    longest = jax.random.randint(jax.random.fold_in(key, 8), (GROUPS, 1), 0, MEMBERS)
    granules = jnp.where(jnp.arange(MEMBERS)[None, :] == longest, MAXMEM // BLOCK, granules)
    return (granules * BLOCK).astype(jnp.int32)


def plant(entries, key, low, high):
    place = [jax.random.randint(jax.random.fold_in(key, axis), (), 0, length) for axis, length in enumerate(entries.shape)]
    main_axis = entries.shape.index(max(entries.shape))
    beside = place[:main_axis] + [(place[main_axis] + 1) % entries.shape[main_axis]] + place[main_axis + 1:]
    return entries.at[tuple(place)].set(low).at[tuple(beside)].set(high)


def steps_of(own_key, shape, cuts, least, largest):
    def one(dim, shards_of):
        draws = jax.random.uniform(jax.random.fold_in(jax.random.fold_in(own_key, 6), dim), (shards_of,), jnp.float32, least / len(cuts), largest / len(cuts))
        return jnp.repeat(jnp.exp(draws), shape[dim] // shards_of).reshape((-1,) + (1,) * (len(shape) - dim - 1))

    factor_of = one(*cuts[0])
    for cut in cuts[1:]:
        factor_of = factor_of * one(*cut)
    return factor_of


def normal_values(rng, extent, scale, limit, cuts=(), kind=jnp.bfloat16):
    loudness = steps_of(rng, extent, cuts, -0.22, 0.18) if cuts else 1.0
    values = jax.random.normal(rng, extent, jnp.float32) * scale * loudness
    return jnp.minimum(jnp.maximum(values, -limit), limit).astype(kind)


def setup_inputs(seed: int = 0) -> dict:
    seeds = jax.random.split(jax.random.key(seed), 10)
    queries = draw_queries(jax.random.fold_in(seeds[9], 71), 0)
    mem_keys = draw_mem_keys(jax.random.fold_in(seeds[9], 71), 0)
    mem_values = normal_values(seeds[2], (GROUPS, MEMBERS, MAXMEM, HEADS * HEAD_DIM), 8.0, 48.0, ((0, 16), (1, 16)))
    lengths = draw_lengths(jax.random.fold_in(seeds[9], 71), 0)
    mates = plant((jax.random.randint(seeds[4], (GROUPS, MEMBERS, MEMBERS), 0, 4) < 3).astype(jnp.int32), jax.random.fold_in(seeds[4], 1), 0, 1)
    out_grad = normal_values(seeds[5], (GROUPS, MEMBERS, Q, HEADS * HEAD_DIM), 1.0, 6.0, ((0, 16), (1, 16)))
    mlp_input = normal_values(seeds[6], (GROUPS, MEMBERS, Q, D), 1.0, 6.0, ((0, 16), (1, 16)))
    gate_pre = normal_values(seeds[7], (GROUPS, MEMBERS, Q, FF), 1.0, 6.0, ((0, 16), (1, 16)))
    hidden_grad = normal_values(seeds[8], (GROUPS, MEMBERS, Q, FF), TOKENS ** -0.5, 0.03125, ((0, 16), (1, 16)))
    return {"queries": queries, "mem_keys": mem_keys, "mem_values": mem_values, "lengths": lengths, "mates": mates, "out_grad": out_grad, "mlp_input": mlp_input, "gate_pre": gate_pre, "hidden_grad": hidden_grad}


def head_pass(query_head, key_head, value_head, grad_head, key_mask):
    inv_root = HEAD_DIM ** -0.5
    scores = jnp.dot(query_head, key_head.T, preferred_element_type=jnp.float32) * inv_root
    scores = jnp.where(key_mask, scores, -1e30)
    highest = jnp.max(scores, axis=1, keepdims=True)
    weights = jnp.exp(scores - highest)
    row_total = jnp.sum(weights, axis=1, keepdims=True)
    weights_bf = (weights / row_total).astype(jnp.bfloat16)
    result = jnp.dot(weights_bf, value_head, preferred_element_type=jnp.float32).astype(jnp.bfloat16)
    grad_weights = jnp.dot(grad_head, value_head.T, preferred_element_type=jnp.float32)
    row_dot = jnp.sum(grad_head.astype(jnp.float32) * result.astype(jnp.float32), axis=1, keepdims=True)
    grad_scores = (weights_bf.astype(jnp.float32) * (grad_weights - row_dot)).astype(jnp.bfloat16)
    grad_query = (jnp.dot(grad_scores, key_head, preferred_element_type=jnp.float32) * inv_root).astype(jnp.bfloat16)
    return result, grad_query


def split_heads(block, row_count):
    return block.reshape(MEMBERS * row_count, HEADS, HEAD_DIM).transpose(1, 0, 2)


def join_heads(block):
    return block.transpose(1, 0, 2).reshape(MEMBERS, Q, HEADS * HEAD_DIM)


def group_pass(inputs):
    query_grp, key_grp, value_grp, grad_grp, length_row, mates_row = inputs
    allowed = (mates_row > 0) | jnp.eye(MEMBERS, dtype=bool)
    live_keys = jnp.arange(MAXMEM, dtype=jnp.int32)[None, :] < length_row[:, None]
    key_mask = jnp.broadcast_to(allowed[:, None, :, None] & live_keys[None, None, :, :], (MEMBERS, Q, MEMBERS, MAXMEM))
    key_mask = key_mask.reshape(MEMBERS * Q, MEMBERS * MAXMEM)

    def one_head(pieces):
        return head_pass(pieces[0], pieces[1], pieces[2], pieces[3], key_mask)

    results, gradients = lax.map(one_head, (split_heads(query_grp, Q), split_heads(key_grp, MAXMEM), split_heads(value_grp, MAXMEM), split_heads(grad_grp, Q)))
    return join_heads(results), join_heads(gradients)


def reference(queries, mem_keys, mem_values, lengths, mates, out_grad, mlp_input, gate_pre, hidden_grad):
    attn_out, q_grad = lax.map(group_pass, (queries, mem_keys, mem_values, out_grad, lengths, mates))

    def add_group(running, triple):
        inputs_grp, cot_grp, gate_grp = triple
        up_cot = (cot_grp.astype(jnp.float32) * jax.nn.silu(gate_grp.astype(jnp.float32))).astype(jnp.bfloat16)
        slab = jnp.dot(inputs_grp.reshape(MEMBERS * Q, D).T, up_cot.reshape(MEMBERS * Q, FF), preferred_element_type=jnp.float32)
        rounded = lax.optimization_barrier(slab.astype(jnp.bfloat16))
        return running + rounded.astype(jnp.float32), None

    up_grad, _ = lax.scan(add_group, jnp.zeros((D, FF), jnp.float32), (mlp_input, hidden_grad, gate_pre))
    return attn_out, q_grad, up_grad
```

```python
import functools
import math

import jax
import jax.numpy as jnp
from jax import lax
from jax.experimental import pallas as pl
from jax.experimental.pallas import tpu as pltpu
from jax.sharding import Mesh
from jax.sharding import PartitionSpec as P


HEAD_DIM = 128
F32 = jnp.float32
BF = jnp.bfloat16
GR = 128
NEG = -1e30
CG = 4
DP = ("x", "zh")
GRP = ("zl", "y", "c")
ZC = ("zl", "c")
AXES = ("zl", "y", "c", "x", "zh")
ANY = pl.BlockSpec(memory_space=pl.ANY)
SMEM = pl.BlockSpec(memory_space=pltpu.SMEM)

def nt(a,b):
    return lax.dot_general(a,b,(((1,),(1,)),((),())),preferred_element_type=F32)

def attn_kernel(members, rows_q, mem_rows, len_ref, mate_ref, x_ref, o_ref, s_ref, p_ref, idx_ref):
    i = pl.program_id(0)
    doc_rows = 2 * rows_q + 2 * mem_rows
    inv_root = 1.0 / math.sqrt(HEAD_DIM)
    scale = inv_root * math.log2(math.e)
    total = members * (mem_rows // GR)
    base = pl.multiple_of(i * doc_rows, 128)
    wide = CG * GR

    n = jnp.int32(0)
    for j in range(members):
        reads = (mate_ref[i, j] > 0) | (i == j)
        for t in range(mem_rows // GR):
            idx_ref[n] = j * doc_rows + rows_q + t * GR
            n = n + (reads & (len_ref[j] > t * GR)).astype(jnp.int32)
    for t in range(CG):
        idx_ref[n + t] = base + rows_q

    def nt(a, b):
        return lax.dot_general(a, b, (((1,), (1,)), ((), ())), preferred_element_type=F32)

    def run(nc):
        q = x_ref[pl.ds(base, rows_q), :]
        g = x_ref[pl.ds(pl.multiple_of(base + rows_q + 2 * mem_rows, 128), rows_q), :]

        def rows(c, off):
            return jnp.concatenate(
                [
                    x_ref[pl.ds(pl.multiple_of(idx_ref[c * CG + t] + off, 128), GR), :]
                    for t in range(CG)
                ],
                axis=0,
            )

        top = None
        for c in range(nc):
            s = nt(q, rows(c, 0))
            if c == nc - 1:
                cut = [s[:, :GR]]
                for t in range(1, CG):
                    bias = jnp.where(c * CG + t < n, 0.0, NEG).astype(F32)
                    cut.append(s[:, t * GR : (t + 1) * GR] + bias)
                s = jnp.concatenate(cut, axis=1)
            s_ref[:, c * wide : (c + 1) * wide] = s
            for t in range(CG):
                m = s[:, t * GR : (t + 1) * GR]
                top = m if top is None else jnp.maximum(top, m)
        m = jnp.max(top, axis=1, keepdims=True)
        out = jnp.zeros((rows_q, HEAD_DIM), F32)
        tot = jnp.zeros((rows_q, GR), F32)
        for c in range(nc):
            e = jnp.exp2((s_ref[:, c * wide : (c + 1) * wide] - m) * scale)
            for t in range(CG):
                tot = tot + e[:, t * GR : (t + 1) * GR]
            p = e.astype(BF)
            p_ref[:, c * wide : (c + 1) * wide] = p
            out = out + jnp.dot(p, rows(c, mem_rows), preferred_element_type=F32)
        recip = 1.0 / jnp.sum(tot, axis=1, keepdims=True)
        ob = (out * recip).astype(BF)
        o_ref[0, 0:rows_q, :] = ob
        r = jnp.sum(g.astype(F32) * ob.astype(F32), axis=1, keepdims=True)
        dq = jnp.zeros((rows_q, HEAD_DIM), F32)
        for c in range(nc):
            dp = nt(g, rows(c, mem_rows))
            ds = (p_ref[:, c * wide : (c + 1) * wide].astype(F32) * (dp - r)).astype(BF)
            dq = dq + jnp.dot(ds, rows(c, 0), preferred_element_type=F32)
        o_ref[0, rows_q : 2 * rows_q, :] = (dq * (recip * inv_root)).astype(BF)

    for nc in range(1, -(-total // CG) + 1):

        @pl.when((n > (nc - 1) * CG) & (n <= nc * CG))
        def _():
            run(nc)


def attention(x, lengths, mates, members, rows_q, mem_rows):
    total = members * (mem_rows // GR)
    width = -(-total // CG) * CG * GR
    spec = pltpu.PrefetchScalarGridSpec(
        num_scalar_prefetch=2,
        grid=(members,),
        in_specs=[pl.BlockSpec(x.shape, lambda i, *_: (0, 0), pipeline_mode=pl.Buffered(1))],
        out_specs=pl.BlockSpec((1, 2 * rows_q, HEAD_DIM), lambda i, *_: (i, 0, 0)),
        scratch_shapes=[
            pltpu.VMEM((rows_q, width), F32),
            pltpu.VMEM((rows_q, width), BF),
            pltpu.SMEM((total + CG + 1,), jnp.int32),
        ],
    )
    return pl.pallas_call(
        functools.partial(attn_kernel, members, rows_q, mem_rows),
        out_shape=jax.ShapeDtypeStruct((members, 2 * rows_q, HEAD_DIM), BF),
        grid_spec=spec,
        name="attn",
    )(lengths, mates, x)


def struct(shape, dtype=BF):
    return jax.ShapeDtypeStruct(shape, dtype)


def cut_input(tokens, zc, parts):
    rows, width = tokens.shape
    step = width // parts

    def kernel(zc_ref, src, *rest):
        outs, sems = rest[:parts], rest[parts]
        copies = []
        for k in range(parts):
            col = pl.multiple_of((zc_ref[0] ^ k) * step, 128)
            copies.append(pltpu.make_async_copy(src.at[:, pl.ds(col, step)], outs[k], sems.at[k]))
        for copy in copies:
            copy.start()
        for copy in copies:
            copy.wait()

    return pl.pallas_call(
        kernel,
        out_shape=[struct((rows, step))] * parts,
        in_specs=[SMEM, ANY],
        out_specs=[ANY] * parts,
        scratch_shapes=[pltpu.SemaphoreType.DMA((parts,))],
        name="cut_input",
    )(zc, tokens)


def make_cot(gate, hidden, y, ny, nz):
    rows, width = gate.shape
    piece = width // (ny * nz)
    chunk = 512 if width % 512 == 0 else 128

    def kernel(y_ref, gate_ref, hidden_ref, *rest):
        outs, buf, sems = rest[:ny], rest[ny], rest[ny + 1]
        for j in range(width // chunk):
            cols = slice(j * chunk, (j + 1) * chunk)
            v = gate_ref[:, cols].astype(F32)
            u = hidden_ref[:, cols].astype(F32) * (v / (1.0 + jnp.exp(-v)))
            buf[cols, :] = u.T.astype(BF)
        copies = []
        for s in range(ny):
            q = lax.rem(y_ref[0] + s, ny)
            for z in range(nz):
                row = pl.multiple_of((z * ny + q) * piece, 16)
                copies.append(
                    pltpu.make_async_copy(
                        buf.at[pl.ds(row, piece)], outs[s].at[pl.ds(z * piece, piece)], sems.at[s, z]
                    )
                )
        for copy in copies:
            copy.start()
        for copy in copies:
            copy.wait()

    vmem = pl.BlockSpec(memory_space=pltpu.VMEM)
    return pl.pallas_call(
        kernel,
        out_shape=[struct((nz * piece, rows))] * ny,
        in_specs=[SMEM, vmem, vmem],
        out_specs=[ANY] * ny,
        scratch_shapes=[pltpu.VMEM((width, rows), BF), pltpu.SemaphoreType.DMA((ny, nz))],
        name="make_cot",
    )(y, gate, hidden)


def product(cots, inputs, x, nx, nzc):
    pairs = len(cots)
    f_rows, rows = cots[0].shape
    width = inputs[0].shape[1]
    step = f_rows // nzc
    part = step // nx

    def kernel(x_ref, *rest):
        cot_refs, in_refs = rest[:pairs], rest[pairs : 2 * pairs]
        outs, acc = rest[2 * pairs : 2 * pairs + nx], rest[2 * pairs + nx]
        lhs = jnp.concatenate([ref[...] for ref in cot_refs], axis=1)
        rhs = jnp.concatenate([ref[...] for ref in in_refs], axis=0)
        acc[...] = jnp.dot(lhs, rhs, preferred_element_type=F32)
        for s in range(nx):
            row = pl.multiple_of(lax.rem(x_ref[0] + s, nx) * part, 8)
            outs[s][0] = acc[pl.ds(row, part), :].astype(BF)

    return pl.pallas_call(
        kernel,
        grid=(nzc,),
        out_shape=[struct((nzc, part, width))] * nx,
        in_specs=[SMEM]
        + [pl.BlockSpec((step, rows), lambda j: (j, 0))] * pairs
        + [pl.BlockSpec((rows, width), lambda j: (0, 0), pipeline_mode=pl.Buffered(1))] * pairs,
        out_specs=[pl.BlockSpec((1, part, width), lambda j: (j, 0, 0))] * nx,
        scratch_shapes=[pltpu.VMEM((step, width), F32)],
        name="product",
    )(x, *cots, *inputs)


def sum_parts(parts, nzh):
    nzc, part, width = parts[0].shape
    rows = part // nzh

    def kernel(*refs):
        out = refs[-1]
        total = refs[0][0].astype(F32)
        for ref in refs[1:-1]:
            total = total + ref[0].astype(F32)
        for h in range(nzh):
            out[h] = total[h * rows : (h + 1) * rows, :].astype(BF)

    return pl.pallas_call(
        kernel,
        grid=(nzc,),
        out_shape=struct((nzc * nzh, rows, width)),
        in_specs=[pl.BlockSpec((1, part, width), lambda j: (j, 0, 0))] * len(parts),
        out_specs=pl.BlockSpec((nzh, rows, width), lambda j: (j, 0, 0)),
        name="sum_parts",
    )(*parts)


def final_sum(pieces, nzh):
    count, rows, width = pieces.shape
    nzc = count // nzh

    def kernel(src, out):
        for a in range(nzc):
            total = src[a * nzh].astype(F32)
            for h in range(1, nzh):
                total = total + src[a * nzh + h].astype(F32)
            out[:, a * width : (a + 1) * width] = total

    return pl.pallas_call(kernel, out_shape=struct((rows, nzc * width), F32), name="final_sum")(pieces)


def pack_heads(queries, keys, values, grads, gates, members):
    rows_q, width = queries.shape
    mem_rows = keys.shape[0]
    doc_rows = 2 * rows_q + 2 * mem_rows
    block = 4

    def kernel(q, k, v, g, *rest):
        out = rest[-1]
        for t in range(block):
            cols = slice(t * HEAD_DIM, (t + 1) * HEAD_DIM)
            out[t, 0:rows_q, :] = q[:, cols]
            out[t, rows_q : rows_q + mem_rows, :] = k[:, cols]
            out[t, rows_q + mem_rows : rows_q + 2 * mem_rows, :] = v[:, cols]
            out[t, rows_q + 2 * mem_rows : doc_rows, :] = g[:, cols]

    def spec(rows):
        return pl.BlockSpec((rows, block * HEAD_DIM), lambda j: (0, j))

    return pl.pallas_call(
        kernel,
        grid=(members // block,),
        out_shape=struct((members, doc_rows, HEAD_DIM)),
        in_specs=[spec(rows_q), spec(mem_rows), spec(mem_rows), spec(rows_q)] + [ANY] * len(gates),
        out_specs=pl.BlockSpec((block, doc_rows, HEAD_DIM), lambda j: (j, 0, 0)),
        name="pack_heads",
    )(queries, keys, values, grads, *gates)


def unpack_heads(pieces, rows_q):
    members = pieces.shape[0]
    block = 4

    def kernel(src, out, grad):
        for t in range(block):
            cols = slice(t * HEAD_DIM, (t + 1) * HEAD_DIM)
            out[:, cols] = src[t, 0:rows_q, :]
            grad[:, cols] = src[t, rows_q : 2 * rows_q, :]

    spec = pl.BlockSpec((rows_q, block * HEAD_DIM), lambda j: (0, j))
    return pl.pallas_call(
        kernel,
        grid=(members // block,),
        out_shape=[struct((rows_q, members * HEAD_DIM))] * 2,
        in_specs=[pl.BlockSpec((block, 2 * rows_q, HEAD_DIM), lambda j: (j, 0, 0))],
        out_specs=[spec, spec],
        name="unpack_heads",
    )(pieces)


def per_device(
    queries, mem_keys, mem_values, lengths, mates, out_grad, mlp_input, gate_pre, hidden_grad
):
    nz, ny, nc = (lax.axis_size(a) for a in GRP)
    nx, nzh = (lax.axis_size(a) for a in DP)
    nzc = nz * nc
    members = nz * ny * nc
    rows_q = queries.shape[2]
    mem_rows = mem_keys.shape[2]
    at_y = lax.axis_index("y").reshape(1).astype(jnp.int32)
    at_x = lax.axis_index("x").reshape(1).astype(jnp.int32)
    at_zc = (lax.axis_index("zl") * nc + lax.axis_index("c")).reshape(1).astype(jnp.int32)

    def swap(v, k):
        return lax.ppermute(v, ZC, [(i, i ^ k) for i in range(nzc)])

    def shift(v, axis, size, s):
        return lax.ppermute(v, axis, [(i, (i + s) % size) for i in range(size)])

    cut = cut_input(mlp_input[0, 0], at_zc, nzc)
    cot = make_cot(gate_pre[0, 0], hidden_grad[0, 0], at_y, ny, nz)

    ins = {}
    for k in range(nzc):
        ins[k, 0] = cut[k] if k == 0 else swap(cut[k], k)
    for k in range(nzc):
        ins[k, 1] = shift(ins[k, 0], "y", ny, 1)
        ins[k, 3] = shift(ins[k, 0], "y", ny, -1)
    for k in range(nzc):
        if k % 2 == 0:
            ins[k, 2] = shift(ins[k, 1], "y", ny, 1)
        else:
            ins[k, 2] = shift(ins[k, 3], "y", ny, -1)

    cots = {}
    for s in range(ny):
        cots[0, s] = cot[s] if s == 0 else shift(cot[s], "y", ny, s)
    for s in range(ny):
        cots[2, s] = swap(cots[0, s], 2)
        cots[1, s] = swap(cots[0, s], 1)
    for s in range(ny):
        cots[3, s] = swap(cots[2, s], 1)

    order = [(k, s) for k in range(nzc) for s in range(ny)]
    parts = product([cots[o] for o in order], [ins[o] for o in order], at_x, nx, nzc)
    parts = [parts[0]] + [shift(parts[s], "x", nx, s) for s in range(1, nx)]
    summed = sum_parts(parts, nzh)
    pieces = lax.all_to_all(summed, ("zl", "c", "zh"), 0, 0, tiled=True)
    up_grad = final_sum(pieces, nzh).T

    gates = [ins[k, s] for k in range(nzc) for s in range(1, ny)] + [
        cots[k, s] for k in range(nzc - 1) for s in range(ny) if (k, s) != (0, 0)
    ]
    packed = pack_heads(
        queries[0, 0], mem_keys[0, 0], mem_values[0, 0], out_grad[0, 0], gates, members
    )
    arrived = lax.all_to_all(packed, GRP, 0, 0, tiled=True)
    heads = attention(arrived.reshape(-1, HEAD_DIM), lengths[0], mates[0], members, rows_q, mem_rows)
    back = lax.all_to_all(heads, GRP, 0, 0, tiled=True)
    attn_out, q_grad = unpack_heads(back, rows_q)
    return (attn_out[None, None], q_grad[None, None], up_grad)


def solution(mesh):
    shape = (2, mesh.shape["grp"] // 4, 2, 4, mesh.shape["dp"] // 4)
    finer = Mesh(mesh.devices.reshape(shape), AXES)
    doc = P(DP, GRP, None, None)
    return jax.shard_map(
        per_device,
        mesh=finer,
        in_specs=(doc, doc, doc, P(DP, None), P(DP, None, None), doc, doc, doc, doc),
        out_specs=(doc, doc, P(None, AXES)),
        check_vma=False,
    )
```

```python
import functools
import math

import jax
import jax.numpy as jnp
from jax import lax
from jax.experimental import pallas as pl
from jax.experimental.pallas import tpu as pltpu
from jax.sharding import Mesh
from jax.sharding import PartitionSpec as P


HEAD_DIM = 128
F32 = jnp.float32
BF = jnp.bfloat16
GR = 128
NEG = -1e30
CG = 4
DP = ("x", "zh")
GRP = ("zl", "y", "c")
ZC = ("zl", "c")
AXES = ("zl", "y", "c", "x", "zh")
ANY = pl.BlockSpec(memory_space=pl.ANY)
SMEM = pl.BlockSpec(memory_space=pltpu.SMEM)

def nt(a,b):
    return lax.dot_general(a,b,(((1,),(1,)),((),())),preferred_element_type=F32)

def attn_kernel(members, rows_q, mem_rows, first, len_ref, mate_ref, x_ref, *rest):
    o_ref, token, s_ref, p_ref, idx_ref = rest[-5:]
    i = pl.program_id(0) + first
    token[...] = jnp.zeros(token.shape, F32)
    doc_rows = 2 * rows_q + 2 * mem_rows
    inv_root = 1.0 / math.sqrt(HEAD_DIM)
    scale = inv_root * math.log2(math.e)
    total = members * (mem_rows // GR)
    base = pl.multiple_of(i * doc_rows, 128)
    wide = CG * GR

    n = jnp.int32(0)
    for t in range(total):
        idx_ref[t] = base + rows_q
    for j in range(members):
        reads = (mate_ref[i, j] > 0) | (i == j)
        for t in range(mem_rows // GR):
            idx_ref[n] = j * doc_rows + rows_q + t * GR
            n = n + (reads & (len_ref[j] > t * GR)).astype(jnp.int32)
    def nt(a, b):
        return lax.dot_general(a, b, (((1,), (1,)), ((), ())), preferred_element_type=F32)

    def run(nc, sure):
        q = x_ref[pl.ds(base, rows_q), :]
        g = x_ref[pl.ds(pl.multiple_of(base + rows_q + 2 * mem_rows, 128), rows_q), :]

        def rows(c, off):
            return jnp.concatenate(
                [
                    x_ref[pl.ds(pl.multiple_of(idx_ref[c * CG + t] + off, 128), GR), :]
                    for t in range(CG)
                ],
                axis=0,
            )

        top = None
        for c in range(nc):
            s = nt(q, rows(c, 0))
            if (c + 1) * CG > sure:
                cut = []
                for t in range(CG):
                    bias = jnp.where(c * CG + t < n, 0.0, NEG).astype(F32)
                    cut.append(s[:, t * GR : (t + 1) * GR] + bias)
                s = jnp.concatenate(cut, axis=1)
            s_ref[:, c * wide : (c + 1) * wide] = s
            for t in range(CG):
                m = s[:, t * GR : (t + 1) * GR]
                top = m if top is None else jnp.maximum(top, m)
        m = jnp.max(top, axis=1, keepdims=True)
        out = jnp.zeros((rows_q, HEAD_DIM), F32)
        tot = jnp.zeros((rows_q, GR), F32)
        for c in range(nc):
            e = jnp.exp2((s_ref[:, c * wide : (c + 1) * wide] - m) * scale)
            for t in range(CG):
                tot = tot + e[:, t * GR : (t + 1) * GR]
            p = e.astype(BF)
            p_ref[:, c * wide : (c + 1) * wide] = p
            out = out + jnp.dot(p, rows(c, mem_rows), preferred_element_type=F32)
        recip = 1.0 / jnp.sum(tot, axis=1, keepdims=True)
        ob = (out * recip).astype(BF)
        o_ref[0, 0:rows_q, :] = ob
        r = jnp.sum(g.astype(F32) * ob.astype(F32), axis=1, keepdims=True)
        dq = jnp.zeros((rows_q, HEAD_DIM), F32)
        for c in range(nc):
            dp = nt(g, rows(c, mem_rows))
            ds = (p_ref[:, c * wide : (c + 1) * wide].astype(F32) * (dp - r)).astype(BF)
            dq = dq + jnp.dot(ds, rows(c, 0), preferred_element_type=F32)
        o_ref[0, rows_q : 2 * rows_q, :] = (dq * (recip * inv_root)).astype(BF)

    most = -(-total // CG)
    counts = [nc for nc in range(1, most + 1) if nc in (most // 2, most * 5 // 8, most * 3 // 4, most)]
    for last, nc in zip([0] + counts[:-1], counts):

        @pl.when((n > last * CG) & (n <= nc * CG))
        def _():
            run(nc, last * CG + 1)


def attention(x, lengths, mates, members, rows_q, mem_rows, first, count, waits, into=None):
    total = members * (mem_rows // GR)
    width = -(-total // CG) * CG * GR
    more = list(waits) + ([] if into is None else [into])
    spec = pltpu.PrefetchScalarGridSpec(
        num_scalar_prefetch=2,
        grid=(count,),
        in_specs=[pl.BlockSpec(x.shape, lambda i, *_: (0, 0), pipeline_mode=pl.Buffered(1))]
        + [ANY] * len(more),
        out_specs=[
            pl.BlockSpec((1, 2 * rows_q, HEAD_DIM), lambda i, *_: (i + first, 0, 0)),
            pl.BlockSpec((8, 128), lambda i, *_: (0, 0)),
        ],
        scratch_shapes=[
            pltpu.VMEM((rows_q, width), F32),
            pltpu.VMEM((rows_q, width), BF),
            pltpu.SMEM((total + 1,), jnp.int32),
        ],
    )
    return pl.pallas_call(
        functools.partial(attn_kernel, members, rows_q, mem_rows, first),
        out_shape=[struct((members, 2 * rows_q, HEAD_DIM)), struct((8, 128), F32)],
        grid_spec=spec,
        input_output_aliases={} if into is None else {2 + len(more): 0},
        name="attn",
    )(lengths, mates, x, *more)


def struct(shape, dtype=BF):
    return jax.ShapeDtypeStruct(shape, dtype)


def cut_input(tokens, zc, parts):
    rows, width = tokens.shape
    step = width // parts

    def kernel(zc_ref, *refs):
        for k in range(parts):
            refs[parts + k][...] = refs[k][...]

    def spec(k):
        return pl.BlockSpec((rows, step), lambda i, zc_ref: (0, zc_ref[0] ^ k))

    grid = pltpu.PrefetchScalarGridSpec(
        num_scalar_prefetch=1,
        grid=(1,),
        in_specs=[spec(k) for k in range(parts)],
        out_specs=[pl.BlockSpec((rows, step), lambda i, zc_ref: (0, 0))] * parts,
    )
    return pl.pallas_call(
        kernel, grid_spec=grid, out_shape=[struct((rows, step))] * parts, name="cut_input"
    )(zc, *([tokens] * parts))


def make_cot(gate, hidden, y, ny, nz):
    rows, width = gate.shape
    piece = width // (ny * nz)
    chunk = 512 if width % 512 == 0 else 128

    def kernel(y_ref, gate_ref, hidden_ref, *rest):
        outs, buf, sems = rest[:ny], rest[ny], rest[ny + 1]
        for j in range(width // chunk):
            cols = slice(j * chunk, (j + 1) * chunk)
            v = gate_ref[:, cols].astype(F32)
            u = hidden_ref[:, cols].astype(F32) * (v / (1.0 + jnp.exp(-v)))
            buf[cols, :] = u.T.astype(BF)
        copies = []
        for s in range(ny):
            q = lax.rem(y_ref[0] + s, ny)
            for z in range(nz):
                row = pl.multiple_of((z * ny + q) * piece, 16)
                copies.append(
                    pltpu.make_async_copy(
                        buf.at[pl.ds(row, piece)], outs[s].at[pl.ds(z * piece, piece)], sems.at[s, z]
                    )
                )
        for copy in copies:
            copy.start()
        for copy in copies:
            copy.wait()

    vmem = pl.BlockSpec(memory_space=pltpu.VMEM)
    return pl.pallas_call(
        kernel,
        out_shape=[struct((nz * piece, rows))] * ny,
        in_specs=[SMEM, vmem, vmem],
        out_specs=[ANY] * ny,
        scratch_shapes=[pltpu.VMEM((width, rows), BF), pltpu.SemaphoreType.DMA((ny, nz))],
        name="make_cot",
    )(y, gate, hidden)


def product(cots, inputs, x, nx, nzc):
    pieces, f_rows, rows = cots[0][0].shape
    width = inputs[0].shape[1]
    step = f_rows // nzc
    part = step // nx
    flat = [v for pair in cots for v in pair]
    tokens = sum(v.shape[0] for v in inputs)

    def kernel(x_ref, *rest):
        cot_refs, in_refs = rest[: len(flat)], rest[len(flat) : len(flat) + len(inputs)]
        rest = rest[len(flat) + len(inputs) :]
        outs, acc, rhs = rest[:nx], rest[nx], rest[nx + 1]

        @pl.when(pl.program_id(0) == 0)
        def _():
            at = 0
            for ref in in_refs:
                rhs[at : at + ref.shape[0], :] = ref[...]
                at += ref.shape[0]

        cols = []
        for low, high in zip(cot_refs[0::2], cot_refs[1::2]):
            cols.append((low, high))
        lhs = []
        for low, high in cols:
            for h in range(pieces):
                lhs += [low[h], high[h]]
        acc[...] = jnp.dot(jnp.concatenate(lhs, axis=1), rhs[...], preferred_element_type=F32)
        for s in range(nx):
            row = pl.multiple_of(lax.rem(x_ref[0] + s, nx) * part, 8)
            outs[s][0] = acc[pl.ds(row, part), :].astype(BF)

    return pl.pallas_call(
        kernel,
        grid=(nzc,),
        out_shape=[struct((nzc, part, width))] * nx,
        in_specs=[SMEM]
        + [pl.BlockSpec((pieces, step, rows), lambda j: (0, j, 0))] * len(flat)
        + [
            pl.BlockSpec(v.shape, lambda j: (0, 0), pipeline_mode=pl.Buffered(1)) for v in inputs
        ],
        out_specs=[pl.BlockSpec((1, part, width), lambda j: (j, 0, 0))] * nx,
        scratch_shapes=[pltpu.VMEM((step, width), F32), pltpu.VMEM((tokens, width), BF)],
        name="product",
    )(x, *flat, *inputs)


def sum_parts(parts, gate, nzh):
    nzc, part, width = parts[0].shape
    rows = part // nzh

    def kernel(*refs):
        out = refs[-1]
        total = refs[0][0].astype(F32)
        for ref in refs[1:-2]:
            total = total + ref[0].astype(F32)
        for h in range(nzh):
            out[h] = total[h * rows : (h + 1) * rows, :].astype(BF)

    return pl.pallas_call(
        kernel,
        grid=(nzc,),
        out_shape=struct((nzc * nzh, rows, width)),
        in_specs=[pl.BlockSpec((1, part, width), lambda j: (j, 0, 0))] * len(parts) + [ANY],
        out_specs=pl.BlockSpec((nzh, rows, width), lambda j: (j, 0, 0)),
        name="sum_parts",
    )(*parts, gate)


def final_sum(pieces, nzh):
    count, rows, width = pieces.shape
    nzc = count // nzh

    def kernel(src, out):
        for a in range(nzc):
            total = src[a * nzh].astype(F32)
            for h in range(1, nzh):
                total = total + src[a * nzh + h].astype(F32)
            out[:, a * width : (a + 1) * width] = total

    return pl.pallas_call(kernel, out_shape=struct((rows, nzc * width), F32), name="final_sum")(pieces)


def pack_heads(queries, keys, values, grads, gates, members):
    rows_q, width = queries.shape
    mem_rows = keys.shape[0]
    doc_rows = 2 * rows_q + 2 * mem_rows
    block = 4

    def kernel(q, k, v, g, *rest):
        out = rest[-1]
        for t in range(block):
            cols = slice(t * HEAD_DIM, (t + 1) * HEAD_DIM)
            out[t, 0:rows_q, :] = q[:, cols]
            out[t, rows_q : rows_q + mem_rows, :] = k[:, cols]
            out[t, rows_q + mem_rows : rows_q + 2 * mem_rows, :] = v[:, cols]
            out[t, rows_q + 2 * mem_rows : doc_rows, :] = g[:, cols]

    def spec(rows):
        return pl.BlockSpec((rows, block * HEAD_DIM), lambda j: (0, j))

    return pl.pallas_call(
        kernel,
        grid=(members // block,),
        out_shape=struct((members, doc_rows, HEAD_DIM)),
        in_specs=[spec(rows_q), spec(mem_rows), spec(mem_rows), spec(rows_q)] + [ANY] * len(gates),
        out_specs=pl.BlockSpec((block, doc_rows, HEAD_DIM), lambda j: (j, 0, 0)),
        name="pack_heads",
    )(queries, keys, values, grads, *gates)


def unpack_heads(pieces, rows_q):
    members = pieces.shape[0]
    block = 4

    def kernel(src, out, grad):
        for t in range(block):
            cols = slice(t * HEAD_DIM, (t + 1) * HEAD_DIM)
            out[:, cols] = src[t, 0:rows_q, :]
            grad[:, cols] = src[t, rows_q : 2 * rows_q, :]

    spec = pl.BlockSpec((rows_q, block * HEAD_DIM), lambda j: (0, j))
    return pl.pallas_call(
        kernel,
        grid=(members // block,),
        out_shape=[struct((rows_q, members * HEAD_DIM))] * 2,
        in_specs=[pl.BlockSpec((block, 2 * rows_q, HEAD_DIM), lambda j: (j, 0, 0))],
        out_specs=[spec, spec],
        name="unpack_heads",
    )(pieces)


def per_device(
    queries, mem_keys, mem_values, lengths, mates, out_grad, mlp_input, gate_pre, hidden_grad
):
    nz, ny, nc = (lax.axis_size(a) for a in GRP)
    nx, nzh = (lax.axis_size(a) for a in DP)
    nzc = nz * nc
    members = nz * ny * nc
    rows_q = queries.shape[2]
    mem_rows = mem_keys.shape[2]
    at_y = lax.axis_index("y").reshape(1).astype(jnp.int32)
    at_x = lax.axis_index("x").reshape(1).astype(jnp.int32)
    at_zc = (lax.axis_index("zl") * nc + lax.axis_index("c")).reshape(1).astype(jnp.int32)

    def swap(v, k):
        return lax.ppermute(v, ZC, [(i, i ^ k) for i in range(nzc)])

    def shift(v, axis, size, s):
        return lax.ppermute(v, axis, [(i, (i + s) % size) for i in range(size)])

    cut = cut_input(mlp_input[0, 0], at_zc, nzc)
    cot = make_cot(gate_pre[0, 0], hidden_grad[0, 0], at_y, ny, nz)

    near = jnp.concatenate([cut[0], swap(cut[1], 1)], axis=0)
    far = jnp.concatenate([swap(cut[2], 2), swap(cut[3], 3)], axis=0)
    ins = {(0, 0): near, (1, 0): far}
    for h in range(2):
        ins[h, 1] = shift(ins[h, 0], "y", ny, 1)
        ins[h, 3] = shift(ins[h, 0], "y", ny, -1)
    ins[0, 2] = shift(ins[0, 1], "y", ny, 1)
    ins[1, 2] = shift(ins[1, 3], "y", ny, -1)

    cots = {}
    moved = [cot[0]] + [shift(cot[s], "y", ny, s) for s in range(1, ny)]
    for h in range(2):
        cots[0, h] = jnp.stack(moved[2 * h : 2 * h + 2])
    for h in range(2):
        cots[2, h] = swap(cots[0, h], 2)
        cots[1, h] = swap(cots[0, h], 1)
    for h in range(2):
        cots[3, h] = swap(cots[2, h], 1)

    pairs = [(cots[2 * h, t], cots[2 * h + 1, t]) for h in range(2) for t in range(2)]
    parts = product(pairs, [ins[h, s] for h in range(2) for s in range(ny)], at_x, nx, nzc)
    parts = [parts[0]] + [shift(parts[s], "x", nx, s) for s in range(1, nx)]

    gates = [ins[h, s] for h in range(2) for s in range(1, ny)] + [
        cots[k, h] for k in range(1, nzc - 1) for h in range(2)
    ]
    packed = pack_heads(
        queries[0, 0], mem_keys[0, 0], mem_values[0, 0], out_grad[0, 0], gates, members
    )
    arrived = lax.all_to_all(packed, GRP, 0, 0, tiled=True).reshape(-1, HEAD_DIM)
    sizes = (members, rows_q, mem_rows)
    half = members // 2
    heads, token = attention(arrived, lengths[0], mates[0], *sizes, 0, half, [])
    summed = sum_parts(parts, token, nzh)
    heads, _ = attention(arrived, lengths[0], mates[0], *sizes, half, half, [summed], heads)
    pieces = lax.all_to_all(summed, ("zl", "c", "zh"), 0, 0, tiled=True)
    up_grad = final_sum(pieces, nzh).T
    back = lax.all_to_all(heads, GRP, 0, 0, tiled=True)
    attn_out, q_grad = unpack_heads(back, rows_q)
    return (attn_out[None, None], q_grad[None, None], up_grad)


def solution(mesh):
    shape = (2, mesh.shape["grp"] // 4, 2, 4, mesh.shape["dp"] // 4)
    finer = Mesh(mesh.devices.reshape(shape), AXES)
    doc = P(DP, GRP, None, None)
    return jax.shard_map(
        per_device,
        mesh=finer,
        in_specs=(doc, doc, doc, P(DP, None), P(DP, None, None), doc, doc, doc, doc),
        out_specs=(doc, doc, P(None, AXES)),
        check_vma=False,
    )
```
